32 devices in a mesh: groups: 2 (over y), det: 4 (over z), blk: 2 (over x), sub: 2 (over core).
Axes of the slice: x: 2, y: 2, z: 4, core: 2. Of those that a mesh axis runs over, the one named last changes fastest.
Arguments:
- tod: float32 [256, 4, 1024], P(('groups', 'det'), None, ('blk', 'sub')), parts along dimension 0, may hold values from -30 to 30
- pixels: int32 [256, 4, 1024], P('groups', 'det', ('blk', 'sub')), parts along dimension 0, may hold values from 0 to 3071
- span_block: int32 [8, 8], P('groups', ('blk', 'sub')), parts along dimension 0, may hold values from 0 to 7
- weight_class: int32 [256], P('groups'), parts along dimension 0, may hold values from 0 to 7
- class_weight: float32 [16], P('groups'), parts along dimension 0, may hold values from 0.25 to 4
Outputs:
- signal_sum: float32 [16, 3072], P(('groups', 'blk'), ('det', 'sub')), parts along dimension 0
- weight_sum: float32 [16, 3072], P(('groups', 'blk'), ('det', 'sub')), parts along dimension 0
- hit_count: float32 [16, 3072], P(('groups', 'blk'), ('det', 'sub')), parts along dimension 0
The draws below stay inside these ranges and needn't reach their ends.
There are 2 independent parts, one for each index of `groups`. The reference program is written for one: setup_inputs(seed, part) draws one part's arguments, and reference() takes and returns one part's arrays. A program takes and returns all parts, laid end to end along the dimension named above; each array names one. Nothing has to cross between parts.
All inputs are finite; a program needn't handle non-finite values.
Results may differ from the reference program's by a relative error of at most 0.005.
Values sent between devices are 32-bit elements; how exact they have to be, the bound alone decides.
No kernel may reach another device: no remote copies, remote signals or barrier semaphores. Data moves between devices by JAX's collectives and lax.ppermute only.
A program may use at most 64 MiB of HBM per device.

```python
import math
import jax
import jax.numpy as jnp
from jax import lax

BLOCK_PIX = 3072
SPAN = 128
NCLASS = 8
NDET = 128
NSEG = 4
SEG = 1024
NCHUNK = 8
NBLOCKS = 8


def shared_integers(key):
    key_base = jax.random.fold_in(key, 29)
    key_perm, key_first, key_second, key_class, key_one, key_two = jax.random.split(key_base, 6)
    block_order = jax.random.permutation(key_perm, NBLOCKS).astype(jnp.int32)
    first_pick = jax.random.randint(key_first, (NSEG, NCHUNK), 0, NBLOCKS, dtype=jnp.int32)
    second_pick = jax.random.randint(key_second, (NSEG, NCHUNK), 0, NBLOCKS, dtype=jnp.int32)
    span_block = block_order[jnp.minimum(first_pick, second_pick)].astype(jnp.int32)
    weight_class = jax.random.randint(key_class, (NDET,), 0, NCLASS, dtype=jnp.int32)
    pick_one = jax.random.randint(key_one, (NDET, NSEG, SEG), 0, BLOCK_PIX, dtype=jnp.int32)
    pick_two = jax.random.randint(key_two, (NDET, NSEG, SEG), 0, BLOCK_PIX, dtype=jnp.int32)
    ranked = jnp.minimum(pick_one, pick_two)
    blocks = jnp.repeat(span_block, SPAN, axis=1)
    shift_block = blocks[None] * 977 * BLOCK_PIX // 3072
    shift_class = weight_class[:, None, None] * 131 * BLOCK_PIX // 3072
    pixels = ((ranked + shift_block + shift_class) % BLOCK_PIX).astype(jnp.int32)
    return (span_block, weight_class, pixels)


def draw_pixels(key, part):
    return shared_integers(key)[2]


def draw_span_block(key, part):
    return shared_integers(key)[0]


def draw_weight_class(key, part):
    return shared_integers(key)[1]


def draw_tod(key, part):
    base = jax.random.fold_in(key, 17)
    key_gain, key_common, key_noise = jax.random.split(base, 3)
    gains = jax.random.uniform(key_gain, (NDET, 1, 1), jnp.float32, 0.5, 1.5)
    common = 3.0 * jax.random.normal(key_common, (1, NSEG, SEG), jnp.float32)
    noise = jax.random.normal(key_noise, (NDET, NSEG, SEG), jnp.float32)
    return jnp.clip(gains * common + noise, -30.0, 30.0)


def setup_inputs(seed: int = 0, part: int = 0) -> dict:
    key_list = jax.random.split(jax.random.key(seed), 6)
    part_splits = jax.random.split(jax.random.fold_in(key_list[5], part), 6)
    tod = draw_tod(jax.random.fold_in(jax.random.fold_in(key_list[5], part), 71), part)
    pixels = draw_pixels(jax.random.fold_in(jax.random.fold_in(key_list[5], part), 71), part)
    span_block = draw_span_block(jax.random.fold_in(jax.random.fold_in(key_list[5], part), 71), part)
    weight_class = draw_weight_class(jax.random.fold_in(jax.random.fold_in(key_list[5], part), 71), part)
    class_weight = jnp.clip(jnp.exp(jax.random.uniform(part_splits[4], (NCLASS,), jnp.float32, math.log(0.25), math.log(4.0))), 0.25, 4.0)
    return {"tod": tod, "pixels": pixels, "span_block": span_block, "weight_class": weight_class, "class_weight": class_weight}


def reference(tod, pixels, span_block, weight_class, class_weight):
    weight = class_weight[weight_class]
    total = jnp.sum(weight)
    common = jnp.sum(weight[:, None, None] * tod, axis=0) / total
    value = (weight[:, None, None] * (tod - common[None])).astype(jnp.bfloat16)
    value = value.astype(jnp.float32)
    weight_low = lax.optimization_barrier(weight.astype(jnp.bfloat16)).astype(jnp.float32)
    blocks = jnp.repeat(span_block, SPAN, axis=1)
    pixel = (blocks[None] * BLOCK_PIX + pixels).astype(jnp.int32).reshape(-1)
    count = NBLOCKS * BLOCK_PIX
    signal_sum = jax.ops.segment_sum(value.reshape(-1), pixel, num_segments=count)
    weight_full = jnp.broadcast_to(weight_low[:, None, None], tod.shape).reshape(-1)
    weight_sum = jax.ops.segment_sum(weight_full, pixel, num_segments=count)
    hit_count = jax.ops.segment_sum(jnp.ones(pixel.shape, jnp.float32), pixel, num_segments=count)
    return (signal_sum.reshape(NBLOCKS, BLOCK_PIX), weight_sum.reshape(NBLOCKS, BLOCK_PIX), hit_count.reshape(NBLOCKS, BLOCK_PIX))
```

```python
import functools

import jax
import jax.numpy as jnp
from jax import lax
from jax.experimental import pallas as pl
from jax.experimental.pallas import tpu as pltpu
from jax.sharding import PartitionSpec as P

BLOCK_PIX = 3072
SPAN = 128
BLK_OWN = 4
VMEM = pltpu.MemorySpace.VMEM
SMEM = pltpu.MemorySpace.SMEM


def partner(index, step, count):
    return index ^ step if count & (count - 1) == 0 else lax.rem(index + step, count)


def source(index, step, count):
    return index ^ step if count & (count - 1) == 0 else lax.rem(index + count - step, count)


def exchange(x, axes, step, count):
    power = count & (count - 1) == 0
    pairs = [(i, i ^ step if power else (i + step) % count) for i in range(count)]
    return lax.ppermute(x, axes, pairs)


def call(kernel, outs, ins, scratch=(), limit=16 << 20, flops=1 << 20, moved=1 << 20):
    return pl.pallas_call(
        kernel,
        out_shape=outs,
        in_specs=[pl.BlockSpec(memory_space=space) for space in ins],
        out_specs=[pl.BlockSpec(memory_space=VMEM) for _ in outs],
        scratch_shapes=list(scratch),
        compiler_params=pltpu.CompilerParams(vmem_limit_bytes=limit),
        cost_estimate=pl.CostEstimate(flops=flops, bytes_accessed=moved, transcendentals=0),
    )


def cut_kernel(count, tod_ref, *outs):
    me = lax.axis_index("det")
    for step, out in enumerate(outs):
        segment = partner(me, step, count)
        for d in range(tod_ref.shape[0]):
            out[pl.ds(d, 1), :] = tod_ref[d, pl.ds(segment, 1), :]


def bin_kernel(count, lanes, upper, pad, rows, group, pix_ref, weight_ref, *refs):
    parts, outs = refs[:count], refs[count : 2 * count]
    value_ref, low_ref, high_ref, scale_ref, total_ref = refs[2 * count :]
    me = lax.axis_index("det")
    held, samples = parts[0].shape
    spans = samples // SPAN
    weight_all = jnp.sum(weight_ref[...], axis=0, keepdims=True)
    common = [jnp.zeros((1, SPAN), jnp.float32) for _ in range(spans)]
    for step in range(count):
        first = pl.multiple_of(source(me, step, count) * held, held)
        weight = weight_ref[pl.ds(first, held), :]
        scale_ref[0, step * held : (step + 1) * held, :] = weight
        for c in range(spans):
            common[c] += jnp.sum(
                weight * parts[step][:, c * SPAN : (c + 1) * SPAN], axis=0, keepdims=True
            )
        for c in range(spans):
            pix = pix_ref[pl.ds(first, held), c * SPAN : (c + 1) * SPAN]
            high = ((pix.astype(jnp.float32) + 0.5) * (1.0 / lanes)).astype(jnp.int32)
            low = pix - high * lanes
            high_ref[c, step * held : (step + 1) * held, :] = high.astype(jnp.float32)
            low_ref[c, step * held : (step + 1) * held, :] = low.astype(jnp.float32)
    for step in range(count):
        weight = scale_ref[0, step * held : (step + 1) * held, :]
        for c in range(spans):
            value_ref[c, step * held : (step + 1) * held, :] = weight * (
                parts[step][:, c * SPAN : (c + 1) * SPAN] - common[c] / weight_all
            )

    tile = 16

    def spread(ref, d, c):
        return ref[c, pl.ds(d, tile, stride=0), :].astype(jnp.bfloat16)

    number = lax.broadcasted_iota(jnp.int32, (tile, SPAN), 0).astype(jnp.float32)
    low_number = [(number + i).astype(jnp.bfloat16) for i in range(0, lanes, tile)]
    one = jnp.ones((tile, SPAN), jnp.bfloat16)
    zero = jnp.zeros((tile, SPAN), jnp.bfloat16)
    for c in range(spans):

        def step(g, acc):
            left, right = [], []
            for u in range(group):
                d = g * group + u
                low = spread(low_ref, d, c)
                high = spread(high_ref, d, c)
                value = spread(value_ref, d, c)
                scale = spread(scale_ref, d, 0)
                right.append(
                    jnp.concatenate([jnp.where(low == n, one, zero) for n in low_number], axis=0)
                )
                hot = [high == n for n in low_number[: pad // tile]]
                left.append(
                    jnp.concatenate(
                        [jnp.where(h, x, zero) for x in (value, scale, one) for h in hot], axis=0
                    )
                )
            return acc + lax.dot_general(
                jnp.concatenate(left, axis=1),
                jnp.concatenate(right, axis=1),
                (((1,), (1,)), ((), ())),
                preferred_element_type=jnp.float32,
            )

        total_ref[c] = lax.fori_loop(
            0, count * held // group, step, jnp.zeros((3 * pad, lanes), jnp.float32)
        )
    for step in range(count):
        first = partner(me, step, count) * rows
        for c in range(spans):
            for q in range(3):
                at = (c * 3 + q) * rows
                outs[step][at : at + rows, :] = total_ref[c, pl.ds(q * pad + first, rows), :]


def place_kernel(count, blks, subs, spans, own, label_ref, *refs):
    parts, outs = refs[:count], refs[count:]
    me = lax.axis_index("det")
    lanes = parts[0].shape[1]
    here = lax.axis_index("blk") * subs + lax.axis_index("sub")
    for step, out in enumerate(outs):
        to = partner(here, step, blks * subs)
        block, sub = to // subs, lax.rem(to, subs)
        number = lax.broadcasted_iota(jnp.int32, (BLK_OWN, lanes), 0) + block * BLK_OWN
        masks = [
            [number == label_ref[source(me, k, count) * spans + c] for c in range(spans)]
            for k in range(count)
        ]
        for q in range(3):
            for r in range(own):
                total = jnp.zeros((BLK_OWN, lanes), jnp.float32)
                for k in range(count):
                    for c in range(spans):
                        row = (c * 3 + q) * subs * own + sub * own + r
                        part = parts[k][pl.ds(row, BLK_OWN, stride=0), :]
                        total += jnp.where(masks[k][c], part, 0.0)
                at = (q * own + r) * BLK_OWN
                out[at : at + BLK_OWN, :] = total


def on_device(tod, pixels, span_block, weight_class, class_weight):
    dets, blks, subs = (lax.axis_size(name) for name in ("det", "blk", "sub"))
    held, _, samples = tod.shape
    detectors = pixels.shape[0]
    spans = samples // SPAN
    width = BLOCK_PIX // (dets * subs)
    lanes = max(n for n in range(1, 129) if width % n == 0)
    own = width // lanes
    upper = BLOCK_PIX // lanes
    pad = -(-upper // 16) * 16
    f32 = jnp.float32

    cut = call(
        functools.partial(cut_kernel, dets),
        [jax.ShapeDtypeStruct((held, samples), f32)] * dets,
        [VMEM],
    )(tod)
    parts = [cut[0]] + [exchange(cut[k], "det", k, dets) for k in range(1, dets)]

    classes = jnp.arange(class_weight.shape[0], dtype=jnp.int32)
    picker = (weight_class[:, None] == classes[None, :]).astype(f32)
    weight = jnp.sum(picker * class_weight[None, :], axis=1)
    weight = jnp.broadcast_to(weight[:, None], (detectors, SPAN))

    rows = subs * own
    shape = jax.ShapeDtypeStruct((spans * 3 * rows, lanes), f32)
    chunks = call(
        functools.partial(bin_kernel, dets, lanes, upper, pad, rows, 4),
        [shape] * dets,
        [VMEM] * (2 + dets),
        [
            pltpu.VMEM((spans, detectors, SPAN), f32),
            pltpu.VMEM((spans, detectors, SPAN), f32),
            pltpu.VMEM((spans, detectors, SPAN), f32),
            pltpu.VMEM((1, detectors, SPAN), f32),
            pltpu.VMEM((spans, 3 * pad, lanes), f32),
        ],
    )(pixels.reshape(detectors, samples), weight, *parts)
    chunks = [chunks[0]] + [exchange(chunks[k], "det", k, dets) for k in range(1, dets)]

    peers = blks * subs
    shape = jax.ShapeDtypeStruct((3 * own * BLK_OWN, lanes), f32)
    placed = call(
        functools.partial(place_kernel, dets, blks, subs, spans, own),
        [shape] * peers,
        [SMEM] + [VMEM] * dets,
    )(span_block.reshape(-1), *chunks)
    total = placed[0]
    for k in range(1, peers):
        total = total + exchange(placed[k], ("blk", "sub"), k, peers)
    total = total.reshape(3, own, BLK_OWN, lanes).transpose(0, 2, 1, 3)
    total = total.reshape(3, BLK_OWN, width)
    return total[0], total[1], total[2]


def solution(mesh):
    placed = (
        P(("groups", "det"), None, ("blk", "sub")),
        P("groups", "det", ("blk", "sub")),
        P("groups", ("blk", "sub")),
        P("groups"),
        P("groups"),
    )
    return jax.shard_map(
        on_device,
        mesh=mesh,
        in_specs=placed,
        out_specs=(P(("groups", "blk"), ("det", "sub")),) * 3,
        check_vma=False,
    )
```

```python
import functools

import jax
import jax.numpy as jnp
from jax import lax
from jax.experimental import pallas as pl
from jax.experimental.pallas import tpu as pltpu
from jax.sharding import PartitionSpec as P

BLOCK_PIX = 3072
SPAN = 128
BLK_OWN = 4
VMEM = pltpu.MemorySpace.VMEM
SMEM = pltpu.MemorySpace.SMEM


def partner(index, step, count):
    return index ^ step if count & (count - 1) == 0 else lax.rem(index + step, count)


def source(index, step, count):
    return index ^ step if count & (count - 1) == 0 else lax.rem(index + count - step, count)


def exchange(x, axes, step, count):
    power = count & (count - 1) == 0
    pairs = [(i, i ^ step if power else (i + step) % count) for i in range(count)]
    return lax.ppermute(x, axes, pairs)


def call(kernel, outs, ins, scratch=(), limit=16 << 20, flops=1 << 20, moved=1 << 20):
    return pl.pallas_call(
        kernel,
        out_shape=outs,
        in_specs=[pl.BlockSpec(memory_space=space) for space in ins],
        out_specs=[pl.BlockSpec(memory_space=VMEM) for _ in outs],
        scratch_shapes=list(scratch),
        compiler_params=pltpu.CompilerParams(vmem_limit_bytes=limit),
        cost_estimate=pl.CostEstimate(flops=flops, bytes_accessed=moved, transcendentals=0),
    )


def cut_kernel(count, tod_ref, *outs):
    me = lax.axis_index("det")
    for step, out in enumerate(outs):
        segment = partner(me, step, count)
        for d in range(tod_ref.shape[0]):
            out[pl.ds(d, 1), :] = tod_ref[d, pl.ds(segment, 1), :]


TILE = 16


def spread(ref, c, d):
    return ref[c, pl.ds(d, TILE, stride=0), :].astype(jnp.bfloat16)


def numbers(count):
    row = lax.broadcasted_iota(jnp.int32, (TILE, SPAN), 0).astype(jnp.float32)
    return [(row + i).astype(jnp.bfloat16) for i in range(0, count, TILE)]


def one_hot_sums(low_ref, high_ref, values, lows, highs, group):
    spans, detectors, _ = low_ref.shape
    low_number, high_number = numbers(lows), numbers(highs)
    one = jnp.ones((TILE, SPAN), jnp.bfloat16)
    zero = jnp.zeros((TILE, SPAN), jnp.bfloat16)

    def step(g, totals):
        sums = []
        for c in range(spans):
            left, right = [], []
            for u in range(group):
                d = g * group + u
                low, high = spread(low_ref, c, d), spread(high_ref, c, d)
                hot = [high == n for n in high_number]
                left.append(
                    jnp.concatenate([jnp.where(low == n, one, zero) for n in low_number], axis=0)
                )
                right.append(
                    jnp.concatenate(
                        [jnp.where(h, v(c, d, one), zero) for v in values for h in hot], axis=0
                    )
                )
            binned = lax.dot_general(
                jnp.concatenate(left, axis=1),
                jnp.concatenate(right, axis=1),
                (((1,), (1,)), ((), ())),
                preferred_element_type=jnp.float32,
            )
            sums.append(binned if totals is None else totals[c] + binned)
        return tuple(sums)

    if detectors == group:
        return step(0, None)
    start = (jnp.zeros((lows, len(values) * highs), jnp.float32),) * spans
    return lax.fori_loop(0, detectors // group, step, start)


def divide(x, by):
    quotient = ((x.astype(jnp.float32) + 0.5) * (1.0 / by)).astype(jnp.int32)
    return quotient, x - quotient * by


def ahead_kernel(lanes, upper, group, pix_ref, weight_ref, sums_ref, half_ref, row_ref, *scratch):
    low_ref, high_ref, scale_ref = scratch
    spans = low_ref.shape[0]
    pad = -(-upper // TILE) * TILE
    scale_ref[0] = weight_ref[...]
    for c in range(spans):
        high, low = divide(pix_ref[:, c * SPAN : (c + 1) * SPAN], lanes)
        side, half = divide(low, lanes // 2)
        low_ref[c] = low.astype(jnp.float32)
        high_ref[c] = high.astype(jnp.float32)
        half_ref[c] = half.astype(jnp.float32)
        row_ref[c] = (side * upper + high).astype(jnp.float32)
    values = [lambda c, d, one: spread(scale_ref, 0, d), lambda c, d, one: one]
    totals = one_hot_sums(low_ref, high_ref, values, lanes, pad, group)
    for c in range(spans):
        turned = totals[c].T
        for q in range(2):
            sums_ref[c, q] = turned[q * pad : q * pad + upper]


def value_kernel(count, lanes, upper, rows, group, weight_ref, sums_ref, half_ref, row_ref, *refs):
    parts, outs = refs[:count], refs[count : 2 * count]
    value_ref, total_ref = refs[2 * count :]
    me = lax.axis_index("det")
    held, samples = parts[0].shape
    spans = samples // SPAN
    weight_all = jnp.sum(weight_ref[...], axis=0, keepdims=True)
    common = [jnp.zeros((1, SPAN), jnp.float32) for _ in range(spans)]
    first = [pl.multiple_of(source(me, k, count) * held, held) for k in range(count)]
    for k in range(count):
        weight = weight_ref[pl.ds(first[k], held), :]
        for c in range(spans):
            part = parts[k][:, c * SPAN : (c + 1) * SPAN]
            common[c] += jnp.sum(weight * part, axis=0, keepdims=True)
    for k in range(count):
        weight = weight_ref[pl.ds(first[k], held), :]
        for c in range(spans):
            part = parts[k][:, c * SPAN : (c + 1) * SPAN]
            value_ref[c, pl.ds(first[k], held), :] = weight * (part - common[c] / weight_all)
    values = [lambda c, d, one: spread(value_ref, c, d)]
    highs = -(-2 * upper // TILE) * TILE
    totals = one_hot_sums(half_ref, row_ref, values, lanes // 2, highs, group)
    for c in range(spans):
        turned = totals[c].T
        total_ref[c, :, : lanes // 2] = turned[:upper]
        total_ref[c, :, lanes // 2 :] = turned[upper : 2 * upper]
    for k in range(count):
        to = partner(me, k, count) * rows
        for c in range(spans):
            at = c * 3 * rows
            outs[k][at : at + rows, :] = total_ref[c, pl.ds(to, rows), :]
            for q in range(2):
                at = (c * 3 + q + 1) * rows
                outs[k][at : at + rows, :] = sums_ref[c, q, pl.ds(to, rows), :]


def place_kernel(count, blks, subs, spans, own, label_ref, *refs):
    parts, outs = refs[:count], refs[count:]
    me = lax.axis_index("det")
    lanes = parts[0].shape[1]
    here = lax.axis_index("blk") * subs + lax.axis_index("sub")
    for step, out in enumerate(outs):
        to = partner(here, step, blks * subs)
        block, sub = to // subs, lax.rem(to, subs)
        number = lax.broadcasted_iota(jnp.int32, (BLK_OWN, lanes), 0) + block * BLK_OWN
        masks = [
            [number == label_ref[source(me, k, count) * spans + c] for c in range(spans)]
            for k in range(count)
        ]
        for q in range(3):
            for r in range(own):
                total = jnp.zeros((BLK_OWN, lanes), jnp.float32)
                for k in range(count):
                    for c in range(spans):
                        row = (c * 3 + q) * subs * own + sub * own + r
                        part = parts[k][pl.ds(row, BLK_OWN, stride=0), :]
                        total += jnp.where(masks[k][c], part, 0.0)
                at = (q * own + r) * BLK_OWN
                out[at : at + BLK_OWN, :] = total


def on_device(tod, pixels, span_block, weight_class, class_weight):
    dets, blks, subs = (lax.axis_size(name) for name in ("det", "blk", "sub"))
    held, _, samples = tod.shape
    detectors = pixels.shape[0]
    spans = samples // SPAN
    width = BLOCK_PIX // (dets * subs)
    lanes = max(n for n in range(1, 129) if width % n == 0)
    own = width // lanes
    upper = BLOCK_PIX // lanes
    f32 = jnp.float32

    cut = call(
        functools.partial(cut_kernel, dets),
        [jax.ShapeDtypeStruct((held, samples), f32)] * dets,
        [VMEM],
    )(tod)
    parts = [cut[0]] + [exchange(cut[k], "det", k, dets) for k in range(1, dets)]

    classes = jnp.arange(class_weight.shape[0], dtype=jnp.int32)
    picker = (weight_class[:, None] == classes[None, :]).astype(f32)
    weight = jnp.sum(picker * class_weight[None, :], axis=1)
    weight = jnp.broadcast_to(weight[:, None], (detectors, SPAN))

    rows = subs * own
    group = min(detectors, 128)
    index = jax.ShapeDtypeStruct((spans, detectors, SPAN), f32)
    held_index = pltpu.VMEM((spans, detectors, SPAN), f32)
    sums, half, row = call(
        functools.partial(ahead_kernel, lanes, upper, min(group, 32)),
        [jax.ShapeDtypeStruct((spans, 2, upper, lanes), f32), index, index],
        [VMEM] * 2,
        [held_index, held_index, pltpu.VMEM((1, detectors, SPAN), f32)],
    )(pixels.reshape(detectors, samples), weight)
    shape = jax.ShapeDtypeStruct((spans * 3 * rows, lanes), f32)
    chunks = call(
        functools.partial(value_kernel, dets, lanes, upper, rows, group),
        [shape] * dets,
        [VMEM] * (4 + dets),
        [held_index, pltpu.VMEM((spans, upper, lanes), f32)],
    )(weight, sums, half, row, *parts)
    chunks = [chunks[0]] + [exchange(chunks[k], "det", k, dets) for k in range(1, dets)]

    peers = blks * subs
    shape = jax.ShapeDtypeStruct((3 * own * BLK_OWN, lanes), f32)
    placed = call(
        functools.partial(place_kernel, dets, blks, subs, spans, own),
        [shape] * peers,
        [SMEM] + [VMEM] * dets,
    )(span_block.reshape(-1), *chunks)
    total = placed[0]
    for k in range(1, peers):
        total = total + exchange(placed[k], ("blk", "sub"), k, peers)
    total = total.reshape(3, own, BLK_OWN, lanes).transpose(0, 2, 1, 3)
    total = total.reshape(3, BLK_OWN, width)
    return total[0], total[1], total[2]


def solution(mesh):
    placed = (
        P(("groups", "det"), None, ("blk", "sub")),
        P("groups", "det", ("blk", "sub")),
        P("groups", ("blk", "sub")),
        P("groups"),
        P("groups"),
    )
    return jax.shard_map(
        on_device,
        mesh=mesh,
        in_specs=placed,
        out_specs=(P(("groups", "blk"), ("det", "sub")),) * 3,
        check_vma=False,
    )
```

```python
import functools

import jax
import jax.numpy as jnp
from jax import lax
from jax.experimental import pallas as pl
from jax.experimental.pallas import tpu as pltpu
from jax.sharding import PartitionSpec as P


BLOCK_PIX = 3072
SPAN = 128
BLK_OWN = 4
XOR = {"tod": True, "bins": False, "maps": True}
VMEM = pltpu.MemorySpace.VMEM


def partner(name, index, step, count):
    return index ^ step if XOR[name] else lax.rem(index + step, count)


def source(name, index, step, count):
    return index ^ step if XOR[name] else lax.rem(index + count - step, count)


def exchange(name, x, axes, step, count):
    power = XOR[name]
    pairs = [(i, i ^ step if power else (i + step) % count) for i in range(count)]
    return lax.ppermute(x, axes, pairs)


def call(kernel, outs, ins, scratch=(), limit=16 << 20, flops=1 << 20, moved=1 << 20):
    return pl.pallas_call(
        kernel,
        out_shape=outs,
        in_specs=[pl.BlockSpec(memory_space=space) for space in ins],
        out_specs=[pl.BlockSpec(memory_space=VMEM) for _ in outs],
        scratch_shapes=list(scratch),
        compiler_params=pltpu.CompilerParams(vmem_limit_bytes=limit),
        cost_estimate=pl.CostEstimate(flops=flops, bytes_accessed=moved, transcendentals=0),
    )


def cut_kernel(count, tod_ref, *outs):
    me = lax.axis_index("det")
    for step, out in enumerate(outs):
        segment = partner("tod", me, step, count)
        for d in range(tod_ref.shape[0]):
            out[pl.ds(d, 1), :] = tod_ref[d, pl.ds(segment, 1), :]


TILE = 16


def spread(ref, c, d):
    return ref[c, pl.ds(d, TILE, stride=0), :].astype(jnp.bfloat16)


def numbers(count):
    row = lax.broadcasted_iota(jnp.int32, (TILE, SPAN), 0).astype(jnp.float32)
    return [(row + i).astype(jnp.bfloat16) for i in range(0, count, TILE)]


def one_hot_sums(low_ref, high_ref, values, lows, highs, group):
    spans, detectors, _ = low_ref.shape
    low_number, high_number = numbers(lows), numbers(highs)
    one = jnp.ones((TILE, SPAN), jnp.bfloat16)
    zero = jnp.zeros((TILE, SPAN), jnp.bfloat16)

    def step(g, totals):
        sums = []
        for c in range(spans):
            left, right = [], []
            for u in range(group):
                d = g * group + u
                low, high = spread(low_ref, c, d), spread(high_ref, c, d)
                hot = [high == n for n in high_number]
                left.append(
                    jnp.concatenate([jnp.where(low == n, one, zero) for n in low_number], axis=0)
                )
                right.append(
                    jnp.concatenate(
                        [jnp.where(h, v(c, d, one), zero) for v in values for h in hot], axis=0
                    )
                )
            binned = lax.dot_general(
                jnp.concatenate(left, axis=1),
                jnp.concatenate(right, axis=1),
                (((1,), (1,)), ((), ())),
                preferred_element_type=jnp.float32,
            )
            sums.append(binned if totals is None else totals[c] + binned)
        return tuple(sums)

    if detectors == group:
        return step(0, None)
    start = (jnp.zeros((lows, len(values) * highs), jnp.float32),) * spans
    return lax.fori_loop(0, detectors // group, step, start)


def divide(x, by):
    quotient = ((x.astype(jnp.float32) + 0.5) * (1.0 / by)).astype(jnp.int32)
    return quotient, x - quotient * by


def ahead_kernel(lanes, upper, group, pix_ref, weight_ref, sums_ref, half_ref, row_ref, *scratch):
    low_ref, high_ref, scale_ref = scratch
    spans = low_ref.shape[0]
    wide = lanes // 4
    pad = -(-wide // TILE) * TILE
    scale_ref[0] = weight_ref[...]
    for c in range(spans):
        row, lane = divide(pix_ref[:, c * SPAN : (c + 1) * SPAN], lanes)
        side, half = divide(lane, 2 * wide)
        quarter, rest = divide(lane, wide)
        low_ref[c] = (quarter * upper + row).astype(jnp.float32)
        high_ref[c] = rest.astype(jnp.float32)
        half_ref[c] = half.astype(jnp.float32)
        row_ref[c] = (side * upper + row).astype(jnp.float32)
    values = [lambda c, d, one: spread(scale_ref, 0, d), lambda c, d, one: one]
    totals = one_hot_sums(low_ref, high_ref, values, 4 * upper, pad, group)
    for c in range(spans):
        for q in range(2):
            for i in range(4):
                part = totals[c][i * upper : (i + 1) * upper, q * pad : q * pad + wide]
                sums_ref[c, q, :, i * wide : (i + 1) * wide] = part


def value_kernel(count, lanes, upper, rows, group, weight_ref, sums_ref, half_ref, row_ref, *refs):
    parts, outs = refs[:count], refs[count : 2 * count]
    value_ref, total_ref = refs[2 * count :]
    me = lax.axis_index("det")
    held, samples = parts[0].shape
    spans = samples // SPAN
    weight_all = jnp.sum(weight_ref[...], axis=0, keepdims=True)
    common = [jnp.zeros((1, SPAN), jnp.float32) for _ in range(spans)]
    first = [pl.multiple_of(source("tod", me, k, count) * held, held) for k in range(count)]
    for k in range(count):
        weight = weight_ref[pl.ds(first[k], held), :]
        for c in range(spans):
            part = parts[k][:, c * SPAN : (c + 1) * SPAN]
            common[c] += jnp.sum(weight * part, axis=0, keepdims=True)
    for k in range(count):
        weight = weight_ref[pl.ds(first[k], held), :]
        for c in range(spans):
            part = parts[k][:, c * SPAN : (c + 1) * SPAN]
            value_ref[c, pl.ds(first[k], held), :] = weight * (part - common[c] / weight_all)
    values = [lambda c, d, one: spread(value_ref, c, d)]
    highs = -(-2 * upper // TILE) * TILE
    totals = one_hot_sums(half_ref, row_ref, values, lanes // 2, highs, group)
    for c in range(spans):
        turned = totals[c].T
        total_ref[c, :, : lanes // 2] = turned[:upper]
        total_ref[c, :, lanes // 2 :] = turned[upper : 2 * upper]
    for k in range(count):
        to = partner("bins", me, k, count) * rows
        for c in range(spans):
            at = c * 3 * rows
            outs[k][at : at + rows, :] = total_ref[c, pl.ds(to, rows), :]
            for q in range(2):
                at = (c * 3 + q + 1) * rows
                outs[k][at : at + rows, :] = sums_ref[c, q, pl.ds(to, rows), :]


def place_kernel(count, blks, subs, spans, own, label_ref, *refs):
    parts, outs, total_ref = refs[:count], refs[count:-1], refs[-1]
    me = lax.axis_index("det")
    blocks, lanes = total_ref.shape[1:]
    here = lax.axis_index("blk") * subs + lax.axis_index("sub")
    number = lax.broadcasted_iota(jnp.int32, (blocks, lanes), 0)
    masks = [
        [
            number == label_ref[pl.ds(source("bins", me, k, count) * spans + c, blocks, stride=0), :]
            for c in range(spans)
        ]
        for k in range(count)
    ]
    rows = 3 * subs * own
    for row in range(rows):
        terms = [
            jnp.where(masks[k][c], parts[k][pl.ds(c * rows + row, blocks, stride=0), :], 0.0)
            for k in range(count)
            for c in range(spans)
        ]
        while len(terms) > 1:
            terms = [sum(terms[i : i + 2]) for i in range(0, len(terms), 2)]
        total_ref[row] = terms[0]
    for step, out in enumerate(outs):
        to = partner("maps", here, step, blks * subs)
        first, sub = to // subs * BLK_OWN, lax.rem(to, subs)
        for q in range(3):
            for r in range(own):
                at = (q * own + r) * BLK_OWN
                row = (q * subs + sub) * own + r
                out[at : at + BLK_OWN, :] = total_ref[row, pl.ds(first, BLK_OWN), :]


def on_device(tod, pixels, span_block, weight_class, class_weight):
    dets, blks, subs = (lax.axis_size(name) for name in ("det", "blk", "sub"))
    held, _, samples = tod.shape
    detectors = pixels.shape[0]
    spans = samples // SPAN
    width = BLOCK_PIX // (dets * subs)
    lanes = max(n for n in range(1, 129) if width % n == 0)
    own = width // lanes
    upper = BLOCK_PIX // lanes
    f32 = jnp.float32

    cut = call(
        functools.partial(cut_kernel, dets),
        [jax.ShapeDtypeStruct((held, samples), f32)] * dets,
        [VMEM],
    )(tod)
    parts = [cut[0]] + [exchange("tod", cut[k], "det", k, dets) for k in range(1, dets)]

    classes = jnp.arange(class_weight.shape[0], dtype=jnp.int32)
    picker = (weight_class[:, None] == classes[None, :]).astype(f32)
    weight = jnp.sum(picker * class_weight[None, :], axis=1)
    weight = jnp.broadcast_to(weight[:, None], (detectors, SPAN))

    rows = subs * own
    group = min(detectors, 128)
    index = jax.ShapeDtypeStruct((spans, detectors, SPAN), f32)
    held_index = pltpu.VMEM((spans, detectors, SPAN), f32)
    sums, half, row = call(
        functools.partial(ahead_kernel, lanes, upper, group),
        [jax.ShapeDtypeStruct((spans, 2, upper, lanes), f32), index, index],
        [VMEM] * 2,
        [held_index, held_index, pltpu.VMEM((1, detectors, SPAN), f32)],
    )(pixels.reshape(detectors, samples), weight)
    shape = jax.ShapeDtypeStruct((spans * 3 * rows, lanes), f32)
    chunks = call(
        functools.partial(value_kernel, dets, lanes, upper, rows, group),
        [shape] * dets,
        [VMEM] * (4 + dets),
        [held_index, pltpu.VMEM((spans, upper, lanes), f32)],
    )(weight, sums, half, row, *parts)
    chunks = [chunks[0]] + [exchange("bins", chunks[k], "det", k, dets) for k in range(1, dets)]

    peers = blks * subs
    shape = jax.ShapeDtypeStruct((3 * own * BLK_OWN, lanes), f32)
    placed = call(
        functools.partial(place_kernel, dets, blks, subs, spans, own),
        [shape] * peers,
        [VMEM] * (1 + dets),
        [pltpu.VMEM((3 * rows, BLK_OWN * blks, lanes), f32)],
    )(jnp.broadcast_to(span_block.reshape(-1, 1), (span_block.size, lanes)), *chunks)
    total = placed[0]
    for k in range(1, peers):
        total = total + exchange("maps", placed[k], ("blk", "sub"), k, peers)
    total = total.reshape(3, own, BLK_OWN, lanes).transpose(0, 2, 1, 3)
    total = total.reshape(3, BLK_OWN, width)
    return total[0], total[1], total[2]


def solution(mesh):
    placed = (
        P(("groups", "det"), None, ("blk", "sub")),
        P("groups", "det", ("blk", "sub")),
        P("groups", ("blk", "sub")),
        P("groups"),
        P("groups"),
    )
    return jax.shard_map(
        on_device,
        mesh=mesh,
        in_specs=placed,
        out_specs=(P(("groups", "blk"), ("det", "sub")),) * 3,
        check_vma=False,
    )
```

```python
import functools

import jax
import jax.numpy as jnp
from jax import lax
from jax.experimental import pallas as pl
from jax.experimental.pallas import tpu as pltpu
from jax.sharding import PartitionSpec as P


BLOCK_PIX = 3072
SPAN = 128
BLK_OWN = 4
XOR = {"tod": True, "bins": False, "maps": True, "label": True}
VMEM = pltpu.MemorySpace.VMEM


def paired(name, count):
    return XOR.get(name, True) and count & (count - 1) == 0


def partner(name, index, step, count):
    return index ^ step if paired(name, count) else lax.rem(index + step, count)


def source(name, index, step, count):
    return index ^ step if paired(name, count) else lax.rem(index + count - step, count)


def exchange(name, x, axes, step, count, inner=1, turn=0):
    pairs = []
    for i in range(count):
        to = i ^ step if paired(name, count) else (i + step) % count
        pairs += [(i * inner + c, to * inner + (c + turn) % inner) for c in range(inner)]
    return lax.ppermute(x, axes, pairs)


def call(kernel, outs, ins, scratch=(), limit=16 << 20, flops=1 << 20, moved=1 << 20):
    return pl.pallas_call(
        kernel,
        out_shape=outs,
        in_specs=[pl.BlockSpec(memory_space=space) for space in ins],
        out_specs=[pl.BlockSpec(memory_space=VMEM) for _ in outs],
        scratch_shapes=list(scratch),
        compiler_params=pltpu.CompilerParams(vmem_limit_bytes=limit),
        cost_estimate=pl.CostEstimate(flops=flops, bytes_accessed=moved, transcendentals=0),
    )


def cut_kernel(count, tod_ref, *outs):
    me = lax.axis_index("det")
    for step, out in enumerate(outs):
        segment = partner("tod", me, step, count)
        for d in range(tod_ref.shape[0]):
            out[pl.ds(d, 1), :] = tod_ref[d, pl.ds(segment, 1), :]


TILE = 16


def spread(ref, c, d):
    return ref[c, pl.ds(d, TILE, stride=0), :].astype(jnp.bfloat16)


def numbers(count):
    row = lax.broadcasted_iota(jnp.int32, (TILE, SPAN), 0).astype(jnp.float32)
    return [(row + i).astype(jnp.bfloat16) for i in range(0, count, TILE)]


def one_hot_sums(low_ref, high_ref, values, lows, highs, group):
    spans, detectors, _ = low_ref.shape
    low_number, high_number = numbers(lows), numbers(highs)
    one = jnp.ones((TILE, SPAN), jnp.bfloat16)
    zero = jnp.zeros((TILE, SPAN), jnp.bfloat16)

    def step(g, totals):
        sums = []
        for c in range(spans):
            left, right = [], []
            for u in range(group):
                d = g * group + u
                low, high = spread(low_ref, c, d), spread(high_ref, c, d)
                hot = [high == n for n in high_number]
                left.append(
                    jnp.concatenate([jnp.where(low == n, one, zero) for n in low_number], axis=0)
                )
                right.append(
                    jnp.concatenate(
                        [jnp.where(h, v(c, d, one), zero) for v in values for h in hot], axis=0
                    )
                )
            binned = lax.dot_general(
                jnp.concatenate(left, axis=1),
                jnp.concatenate(right, axis=1),
                (((1,), (1,)), ((), ())),
                preferred_element_type=jnp.float32,
            )
            sums.append(binned if totals is None else totals[c] + binned)
        return tuple(sums)

    if detectors == group:
        return step(0, None)
    start = (jnp.zeros((lows, len(values) * highs), jnp.float32),) * spans
    return lax.fori_loop(0, detectors // group, step, start)


def divide(x, by):
    quotient = ((x.astype(jnp.float32) + 0.5) * (1.0 / by)).astype(jnp.int32)
    return quotient, x - quotient * by


def ahead_kernel(lanes, upper, group, pix_ref, weight_ref, sums_ref, half_ref, row_ref, *scratch):
    low_ref, high_ref, scale_ref = scratch
    spans = low_ref.shape[0]
    wide = lanes // 4
    pad = -(-wide // TILE) * TILE
    scale_ref[0] = weight_ref[...]
    for c in range(spans):
        row, lane = divide(pix_ref[:, c * SPAN : (c + 1) * SPAN], lanes)
        side, half = divide(lane, 2 * wide)
        quarter, rest = divide(lane, wide)
        low_ref[c] = (quarter * upper + row).astype(jnp.float32)
        high_ref[c] = rest.astype(jnp.float32)
        half_ref[c] = half.astype(jnp.float32)
        row_ref[c] = (side * upper + row).astype(jnp.float32)
    values = [lambda c, d, one: spread(scale_ref, 0, d), lambda c, d, one: one]
    totals = one_hot_sums(low_ref, high_ref, values, 4 * upper, pad, group)
    for c in range(spans):
        for q in range(2):
            for i in range(4):
                part = totals[c][i * upper : (i + 1) * upper, q * pad : q * pad + wide]
                sums_ref[c, q, :, i * wide : (i + 1) * wide] = part


def value_kernel(count, lanes, upper, rows, group, weight_ref, sums_ref, half_ref, row_ref, *refs):
    parts, outs = refs[:count], refs[count : 2 * count]
    value_ref, total_ref = refs[2 * count :]
    me = lax.axis_index("det")
    held, samples = parts[0].shape
    spans = samples // SPAN
    weight_all = jnp.sum(weight_ref[...], axis=0, keepdims=True)
    common = [jnp.zeros((1, SPAN), jnp.float32) for _ in range(spans)]
    first = [pl.multiple_of(source("tod", me, k, count) * held, held) for k in range(count)]
    for k in range(count):
        weight = weight_ref[pl.ds(first[k], held), :]
        for c in range(spans):
            part = parts[k][:, c * SPAN : (c + 1) * SPAN]
            common[c] += jnp.sum(weight * part, axis=0, keepdims=True)
    for k in range(count):
        weight = weight_ref[pl.ds(first[k], held), :]
        for c in range(spans):
            part = parts[k][:, c * SPAN : (c + 1) * SPAN]
            value_ref[c, pl.ds(first[k], held), :] = weight * (part - common[c] / weight_all)
    values = [lambda c, d, one: spread(value_ref, c, d)]
    highs = -(-2 * upper // TILE) * TILE
    totals = one_hot_sums(half_ref, row_ref, values, lanes // 2, highs, group)
    for c in range(spans):
        turned = totals[c].T
        total_ref[c, :, : lanes // 2] = turned[:upper]
        total_ref[c, :, lanes // 2 :] = turned[upper : 2 * upper]
    for k in range(count):
        to = partner("bins", me, k, count) * rows
        for c in range(spans):
            at = c * 3 * rows
            outs[k][at : at + rows, :] = total_ref[c, pl.ds(to, rows), :]
            for q in range(2):
                at = (c * 3 + q + 1) * rows
                outs[k][at : at + rows, :] = sums_ref[c, q, pl.ds(to, rows), :]


def place_kernel(count, blks, subs, spans, own, label_ref, other_ref, *refs):
    parts, outs, total_ref = refs[:count], refs[count:-1], refs[-1]
    me = lax.axis_index("det")
    blocks, lanes = total_ref.shape[1:]
    number = lax.broadcasted_iota(jnp.int32, (blocks, lanes), 0).astype(jnp.float32)
    masks = []
    for k in range(count):
        labels, first = (other_ref if k else label_ref), source("bins", me, k, count) * spans
        masks.append(
            [number == labels[pl.ds(first + c, blocks, stride=0), :] for c in range(spans)]
        )
    rows = 3 * subs * own
    for row in range(rows):
        terms = [
            jnp.where(masks[k][c], parts[k][pl.ds(c * rows + row, blocks, stride=0), :], 0.0)
            for k in range(count)
            for c in range(spans)
        ]
        while len(terms) > 1:
            terms = [sum(terms[i : i + 2]) for i in range(0, len(terms), 2)]
        total_ref[row] = terms[0]
    for step, out in enumerate(outs):
        first = partner("maps", lax.axis_index("blk"), step, blks) * BLK_OWN
        for h in range(subs):
            sub = lax.rem(lax.axis_index("sub") + (1 if step else 0) + h, subs)
            for q in range(3):
                for r in range(own):
                    at = ((h * 3 + q) * own + r) * BLK_OWN
                    row = (q * subs + sub) * own + r
                    out[at : at + BLK_OWN, :] = total_ref[row, pl.ds(first, BLK_OWN), :]


def on_device(tod, pixels, span_block, weight_class, class_weight):
    dets, blks, subs = (lax.axis_size(name) for name in ("det", "blk", "sub"))
    held, _, samples = tod.shape
    detectors = pixels.shape[0]
    spans = samples // SPAN
    width = BLOCK_PIX // (dets * subs)
    lanes = max(n for n in range(1, 129) if width % n == 0)
    own = width // lanes
    upper = BLOCK_PIX // lanes
    f32 = jnp.float32

    cut = call(
        functools.partial(cut_kernel, dets),
        [jax.ShapeDtypeStruct((held, samples), f32)] * dets,
        [VMEM],
    )(tod)
    parts = [cut[0]] + [exchange("tod", cut[k], "det", k, dets) for k in range(1, dets)]

    classes = jnp.arange(class_weight.shape[0], dtype=jnp.int32)
    picker = (weight_class[:, None] == classes[None, :]).astype(f32)
    weight = jnp.sum(picker * class_weight[None, :], axis=1)
    weight = jnp.broadcast_to(weight[:, None], (detectors, SPAN))

    rows = subs * own
    group = min(detectors, 128)
    index = jax.ShapeDtypeStruct((spans, detectors, SPAN), f32)
    held_index = pltpu.VMEM((spans, detectors, SPAN), f32)
    sums, half, row = call(
        functools.partial(ahead_kernel, lanes, upper, group),
        [jax.ShapeDtypeStruct((spans, 2, upper, lanes), f32), index, index],
        [VMEM] * 2,
        [held_index, held_index, pltpu.VMEM((1, detectors, SPAN), f32)],
    )(pixels.reshape(detectors, samples), weight)
    shape = jax.ShapeDtypeStruct((spans * 3 * rows, lanes), f32)
    chunks = call(
        functools.partial(value_kernel, dets, lanes, upper, rows, group),
        [shape] * dets,
        [VMEM] * (4 + dets),
        [held_index, pltpu.VMEM((spans, upper, lanes), f32)],
    )(weight, sums, half, row, *parts)
    label = span_block.reshape(-1, 1).astype(f32)
    label = jnp.broadcast_to(label, (span_block.size, lanes))
    other = exchange("label", label, ("det", "sub"), 0, dets, subs, 1)
    chunks = [chunks[0]] + [
        exchange("bins", chunks[k], ("det", "sub"), k, dets, subs, -1) for k in range(1, dets)
    ]

    shape = jax.ShapeDtypeStruct((subs * 3 * own * BLK_OWN, lanes), f32)
    placed = call(
        functools.partial(place_kernel, dets, blks, subs, spans, own),
        [shape] * blks,
        [VMEM] * (2 + dets),
        [pltpu.VMEM((3 * rows, BLK_OWN * blks, lanes), f32)],
    )(label, other, *chunks)
    total = placed[0]
    for k in range(1, blks):
        total = total + exchange("maps", placed[k], ("blk", "sub"), k, blks, subs, 1)
    shares = jnp.split(total, subs)
    total = shares[0]
    for h in range(1, subs):
        total = total + exchange(f"swap{h}", shares[h], ("blk", "sub"), 0, blks, subs, h)
    total = total.reshape(3, own, BLK_OWN, lanes).transpose(0, 2, 1, 3)
    total = total.reshape(3, BLK_OWN, width)
    return total[0], total[1], total[2]


def solution(mesh):
    placed = (
        P(("groups", "det"), None, ("blk", "sub")),
        P("groups", "det", ("blk", "sub")),
        P("groups", ("blk", "sub")),
        P("groups"),
        P("groups"),
    )
    return jax.shard_map(
        on_device,
        mesh=mesh,
        in_specs=placed,
        out_specs=(P(("groups", "blk"), ("det", "sub")),) * 3,
        check_vma=False,
    )
```

```python
import functools

import jax
import jax.numpy as jnp
from jax import lax
from jax.experimental import pallas as pl
from jax.experimental.pallas import tpu as pltpu
from jax.sharding import PartitionSpec as P


BLOCK_PIX = 3072
SPAN = 128
BLK_OWN = 4
XOR = {"tod": True, "bins": False, "maps": True}
VMEM = pltpu.MemorySpace.VMEM


def partner(name, index, step, count):
    return index ^ step if XOR[name] else lax.rem(index + step, count)


def source(name, index, step, count):
    return index ^ step if XOR[name] else lax.rem(index + count - step, count)


def exchange(name, x, axes, step, count):
    power = XOR[name]
    pairs = [(i, i ^ step if power else (i + step) % count) for i in range(count)]
    return lax.ppermute(x, axes, pairs)


def call(kernel, outs, ins, scratch=(), limit=16 << 20, flops=1 << 20, moved=1 << 20):
    return pl.pallas_call(
        kernel,
        out_shape=outs,
        in_specs=[pl.BlockSpec(memory_space=space) for space in ins],
        out_specs=[pl.BlockSpec(memory_space=VMEM) for _ in outs],
        scratch_shapes=list(scratch),
        compiler_params=pltpu.CompilerParams(vmem_limit_bytes=limit),
        cost_estimate=pl.CostEstimate(flops=flops, bytes_accessed=moved, transcendentals=0),
    )


def cut_kernel(count, tod_ref, *outs):
    me = lax.axis_index("det")
    for step, out in enumerate(outs):
        segment = partner("tod", me, step, count)
        for d in range(tod_ref.shape[0]):
            out[pl.ds(d, 1), :] = tod_ref[d, pl.ds(segment, 1), :]


TILE = 16


def spread(ref, c, d):
    return ref[c, pl.ds(d, TILE, stride=0), :].astype(jnp.bfloat16)


def numbers(count):
    row = lax.broadcasted_iota(jnp.int32, (TILE, SPAN), 0).astype(jnp.float32)
    return [(row + i).astype(jnp.bfloat16) for i in range(0, count, TILE)]


def one_hot_sums(low_ref, high_ref, values, lows, highs, group):
    spans, detectors, _ = low_ref.shape
    low_number, high_number = numbers(lows), numbers(highs)
    one = jnp.ones((TILE, SPAN), jnp.bfloat16)
    zero = jnp.zeros((TILE, SPAN), jnp.bfloat16)

    def step(g, totals):
        sums = []
        for c in range(spans):
            left, right = [], []
            for u in range(group):
                d = g * group + u
                low, high = spread(low_ref, c, d), spread(high_ref, c, d)
                hot = [high == n for n in high_number]
                left.append(
                    jnp.concatenate([jnp.where(low == n, one, zero) for n in low_number], axis=0)
                )
                right.append(
                    jnp.concatenate(
                        [jnp.where(h, v(c, d, one), zero) for v in values for h in hot], axis=0
                    )
                )
            binned = lax.dot_general(
                jnp.concatenate(left, axis=1),
                jnp.concatenate(right, axis=1),
                (((1,), (1,)), ((), ())),
                preferred_element_type=jnp.float32,
            )
            sums.append(binned if totals is None else totals[c] + binned)
        return tuple(sums)

    if detectors == group:
        return step(0, None)
    start = (jnp.zeros((lows, len(values) * highs), jnp.float32),) * spans
    return lax.fori_loop(0, detectors // group, step, start)


def divide(x, by):
    quotient = ((x.astype(jnp.float32) + 0.5) * (1.0 / by)).astype(jnp.int32)
    return quotient, x - quotient * by


def ahead_kernel(lanes, upper, group, pix_ref, weight_ref, sums_ref, half_ref, row_ref, *scratch):
    low_ref, high_ref, scale_ref = scratch
    spans = low_ref.shape[0]
    wide = lanes // 4
    pad = -(-wide // TILE) * TILE
    scale_ref[0] = weight_ref[...]
    for c in range(spans):
        row, lane = divide(pix_ref[:, c * SPAN : (c + 1) * SPAN], lanes)
        side, half = divide(lane, 2 * wide)
        quarter, rest = divide(lane, wide)
        low_ref[c] = (quarter * upper + row).astype(jnp.float32)
        high_ref[c] = rest.astype(jnp.float32)
        half_ref[c] = half.astype(jnp.float32)
        row_ref[c] = (side * upper + row).astype(jnp.float32)
    values = [lambda c, d, one: spread(scale_ref, 0, d), lambda c, d, one: one]
    totals = one_hot_sums(low_ref, high_ref, values, 4 * upper, pad, group)
    for c in range(spans):
        for q in range(2):
            for i in range(4):
                part = totals[c][i * upper : (i + 1) * upper, q * pad : q * pad + wide]
                sums_ref[c, q, :, i * wide : (i + 1) * wide] = part


def value_kernel(count, lanes, upper, rows, group, weight_ref, sums_ref, half_ref, row_ref, *refs):
    parts, outs = refs[:count], refs[count : 2 * count]
    value_ref, total_ref = refs[2 * count :]
    me = lax.axis_index("det")
    held, samples = parts[0].shape
    spans = samples // SPAN
    weight_all = jnp.sum(weight_ref[...], axis=0, keepdims=True)
    common = [jnp.zeros((1, SPAN), jnp.float32) for _ in range(spans)]
    first = [pl.multiple_of(source("tod", me, k, count) * held, held) for k in range(count)]
    for k in range(count):
        weight = weight_ref[pl.ds(first[k], held), :]
        for c in range(spans):
            part = parts[k][:, c * SPAN : (c + 1) * SPAN]
            common[c] += jnp.sum(weight * part, axis=0, keepdims=True)
    for k in range(count):
        weight = weight_ref[pl.ds(first[k], held), :]
        for c in range(spans):
            part = parts[k][:, c * SPAN : (c + 1) * SPAN]
            value_ref[c, pl.ds(first[k], held), :] = weight * (part - common[c] / weight_all)
    values = [lambda c, d, one: spread(value_ref, c, d)]
    highs = -(-2 * upper // TILE) * TILE
    totals = one_hot_sums(half_ref, row_ref, values, lanes // 2, highs, group)
    for c in range(spans):
        turned = totals[c].T
        total_ref[c, :, : lanes // 2] = turned[:upper]
        total_ref[c, :, lanes // 2 :] = turned[upper : 2 * upper]
    for k in range(count):
        to = partner("bins", me, k, count) * rows
        for c in range(spans):
            at = c * 3 * rows
            outs[k][at : at + rows, :] = total_ref[c, pl.ds(to, rows), :]
            for q in range(2):
                at = (c * 3 + q + 1) * rows
                outs[k][at : at + rows, :] = sums_ref[c, q, pl.ds(to, rows), :]


def place_kernel(count, blks, subs, spans, own, label_ref, *refs):
    parts, outs, total_ref = refs[:count], refs[count:-1], refs[-1]
    me = lax.axis_index("det")
    blocks, lanes = total_ref.shape[1:]
    here = lax.axis_index("blk") * subs + lax.axis_index("sub")
    number = lax.broadcasted_iota(jnp.int32, (blocks, lanes), 0)
    masks = [
        [
            number == label_ref[pl.ds(source("bins", me, k, count) * spans + c, blocks, stride=0), :]
            for c in range(spans)
        ]
        for k in range(count)
    ]
    rows = 3 * subs * own
    for row in range(rows):
        terms = [
            jnp.where(masks[k][c], parts[k][pl.ds(c * rows + row, blocks, stride=0), :], 0.0)
            for k in range(count)
            for c in range(spans)
        ]
        while len(terms) > 1:
            terms = [sum(terms[i : i + 2]) for i in range(0, len(terms), 2)]
        total_ref[row] = terms[0]
    for step, out in enumerate(outs):
        to = partner("maps", here, step, blks * subs)
        first, sub = to // subs * BLK_OWN, lax.rem(to, subs)
        for q in range(3):
            for r in range(own):
                row = (q * subs + sub) * own + r
                out[q * own + r] = total_ref[row, pl.ds(first, BLK_OWN), :]


def on_device(tod, pixels, span_block, weight_class, class_weight):
    dets, blks, subs = (lax.axis_size(name) for name in ("det", "blk", "sub"))
    held, _, samples = tod.shape
    detectors = pixels.shape[0]
    spans = samples // SPAN
    width = BLOCK_PIX // (dets * subs)
    lanes = max(n for n in range(1, 129) if width % n == 0)
    own = width // lanes
    upper = BLOCK_PIX // lanes
    f32 = jnp.float32

    cut = call(
        functools.partial(cut_kernel, dets),
        [jax.ShapeDtypeStruct((held, samples), f32)] * dets,
        [VMEM],
    )(tod)
    parts = [cut[0]] + [exchange("tod", cut[k], "det", k, dets) for k in range(1, dets)]

    classes = jnp.arange(class_weight.shape[0], dtype=jnp.int32)
    picker = (weight_class[:, None] == classes[None, :]).astype(f32)
    weight = jnp.sum(picker * class_weight[None, :], axis=1)
    weight = jnp.broadcast_to(weight[:, None], (detectors, SPAN))

    rows = subs * own
    group = min(detectors, 128)
    index = jax.ShapeDtypeStruct((spans, detectors, SPAN), f32)
    held_index = pltpu.VMEM((spans, detectors, SPAN), f32)
    sums, half, row = call(
        functools.partial(ahead_kernel, lanes, upper, group),
        [jax.ShapeDtypeStruct((spans, 2, upper, lanes), f32), index, index],
        [VMEM] * 2,
        [held_index, held_index, pltpu.VMEM((1, detectors, SPAN), f32)],
    )(pixels.reshape(detectors, samples), weight)
    shape = jax.ShapeDtypeStruct((spans * 3 * rows, lanes), f32)
    chunks = call(
        functools.partial(value_kernel, dets, lanes, upper, rows, group),
        [shape] * dets,
        [VMEM] * (4 + dets),
        [held_index, pltpu.VMEM((spans, upper, lanes), f32)],
    )(weight, sums, half, row, *parts)
    chunks = [chunks[0]] + [exchange("bins", chunks[k], "det", k, dets) for k in range(1, dets)]

    peers = blks * subs
    shape = jax.ShapeDtypeStruct((3 * own, BLK_OWN, lanes), f32)
    placed = call(
        functools.partial(place_kernel, dets, blks, subs, spans, own),
        [shape] * peers,
        [VMEM] * (1 + dets),
        [pltpu.VMEM((3 * rows, BLK_OWN * blks, lanes), f32)],
    )(jnp.broadcast_to(span_block.reshape(-1, 1), (span_block.size, lanes)), *chunks)
    total = placed[0]
    for k in range(1, peers):
        total = total + exchange("maps", placed[k], ("blk", "sub"), k, peers)
    total = total.reshape(3, own, BLK_OWN, lanes).transpose(0, 2, 1, 3)
    total = total.reshape(3, BLK_OWN, width)
    return total[0], total[1], total[2]


def solution(mesh):
    placed = (
        P(("groups", "det"), None, ("blk", "sub")),
        P("groups", "det", ("blk", "sub")),
        P("groups", ("blk", "sub")),
        P("groups"),
        P("groups"),
    )
    return jax.shard_map(
        on_device,
        mesh=mesh,
        in_specs=placed,
        out_specs=(P(("groups", "blk"), ("det", "sub")),) * 3,
        check_vma=False,
    )
```
